32 devices in a mesh: tm: 8 (over z, x), feat: 4 (over y, core).
Axes of the slice: x: 2, y: 2, z: 4, core: 2. Of those that a mesh axis runs over, the one named last changes fastest.
Arguments:
- coords: float32 [512, 3, 8, 256], P('tm'), may hold values from -12 to 12, as said below
- set_a: int32 [128], replicated, may hold values from 0 to 255
- set_b: int32 [128], replicated, may hold values from 0 to 255
Outputs:
- c00: float32 [16384, 16384], P('feat', 'tm')
- c0t: float32 [16384, 16384], P('feat', 'tm')
The draws below stay inside these ranges and needn't reach their ends.
Inputs may be any that keep to these rules, and one draw needn't show every extreme that they name: `coords`: positions of a folding protein.
All inputs are finite; a program needn't handle non-finite values.
Results may differ from the reference program's by a relative error of at most 0.0003.
Values may be sent and summed in bfloat16 or wider, within the bound.
A program may use at most 128 MiB of HBM per device.

```python
import jax
import jax.numpy as jnp
from jax import lax

RES = 256
ATOMS = 8
NA = 128
NB = 128
LAG = 64
FR_DEV = 64
FRAMES = 512


def draw_coords(key, part):
    keys = jax.random.split(key, 5)
    centers = jax.random.normal(keys[0], (3, 1, RES), jnp.float32) * 0.9
    offsets = jax.random.normal(keys[1], (3, ATOMS, RES), jnp.float32) * 0.2
    relax = jnp.exp(jax.random.uniform(keys[2], (1, ATOMS, RES), jnp.float32, 0.0, jnp.log(512.0)))
    factor = jnp.exp(-1.0 / relax)
    noise = jax.random.normal(keys[3], (FRAMES, 3, ATOMS, RES), jnp.float32)
    jitter = jax.random.normal(keys[4], (FRAMES, 3, ATOMS, RES), jnp.float32) * 0.3
    spread = 0.3
    ramp = 1.5 - 0.8 * jnp.arange(FRAMES, dtype=jnp.float32) / max(FRAMES - 1, 1)
    kick = jnp.sqrt(1.0 - factor * factor) * spread

    def advance(state, fresh):
        updated = factor * state + kick * fresh
        return (updated, updated)
    start = noise[0] * spread
    final_state, moves = lax.scan(advance, start, noise)
    positions = ramp[:, None, None, None] * centers[None] + offsets[None] + moves + jitter
    return jnp.clip(positions, -12.0, 12.0).astype(jnp.float32)


def touch_ends(array, key, least, top_value):
    extent = array.shape
    place = [jax.random.randint(jax.random.fold_in(key, axis), (), 0, extent[axis]) for axis in range(len(extent))]
    array = array.at[tuple(place)].set(least)
    longest = extent.index(max(extent))
    place[longest] = (place[longest] + 1) % extent[longest]
    return array.at[tuple(place)].set(top_value)


def setup_inputs(seed: int = 0) -> dict:
    key_of = jax.random.split(jax.random.key(seed), 4)
    coords = draw_coords(jax.random.fold_in(key_of[3], 71), 0)
    set_a = touch_ends(jax.random.randint(key_of[1], (NA,), 0, RES), jax.random.fold_in(key_of[1], 1), 0, RES - 1).astype(jnp.int32)
    set_b = touch_ends(jax.random.randint(key_of[2], (NB,), 0, RES), jax.random.fold_in(key_of[2], 1), 0, RES - 1).astype(jnp.int32)
    return dict(coords=coords, set_a=set_a, set_b=set_b)


contact_radius = 1.2
contact_width = 0.25

def contact_features(positions, index_a, index_b):
    part_a = jnp.take(positions, index_a, axis=3)
    part_b = jnp.take(positions, index_b, axis=3)
    frame_rows = positions.shape[0]
    summed = jnp.zeros((frame_rows, part_a.shape[3], part_b.shape[3]), jnp.float32)
    for first_atom in range(part_a.shape[2]):
        square = jnp.zeros((frame_rows, part_b.shape[2], part_a.shape[3], part_b.shape[3]), jnp.float32)
        for component in range(3):
            difference = part_a[:, component, first_atom, :][:, None, :, None] - part_b[:, component, :, :][:, :, None, :]
            square = square + difference * difference
        summed = summed + lax.optimization_barrier(jnp.sum(jax.nn.sigmoid((contact_radius - jnp.sqrt(square)) / contact_width), axis=1))
    summed = summed / float(part_a.shape[2])
    return summed.reshape(frame_rows, part_a.shape[3] * part_b.shape[3])

def contract_frames(left, right):
    return lax.dot_general(left.astype(jnp.float32), right.astype(jnp.float32), (((0,), (0,)), ((), ())), precision=lax.Precision.HIGHEST, preferred_element_type=jnp.float32)

def reference(coords, set_a, set_b):
    blocks = coords.reshape(FRAMES // FR_DEV, FR_DEV, 3, ATOMS, RES)
    lifted = lax.map(lambda block: contact_features(block, set_a, set_b), blocks).reshape(FRAMES, NA * NB)
    pairs = FRAMES - LAG
    frame_ids = jnp.arange(FRAMES, dtype=jnp.int32)
    weight = (frame_ids < pairs).astype(jnp.float32) + (frame_ids >= LAG).astype(jnp.float32)
    means = jnp.dot(weight, lifted, precision=lax.Precision.HIGHEST) / (2.0 * pairs)
    centered = (lifted - means[None, :]).astype(jnp.bfloat16)
    centered = lax.optimization_barrier(centered)
    early = centered[:pairs].astype(jnp.float32)
    later = centered[LAG:].astype(jnp.float32)
    plus = (early + later).astype(jnp.bfloat16)
    minus = (early - later).astype(jnp.bfloat16)
    sum_plus = contract_frames(plus, plus)
    sum_minus = contract_frames(minus, minus)
    c00 = (sum_plus + sum_minus) / (4.0 * pairs)
    c0t = (sum_plus - sum_minus) / (4.0 * pairs)
    return (c00, c0t)
```

```python
import functools

import jax
import jax.numpy as jnp
from jax import lax
from jax.experimental import pallas as pl
from jax.experimental.pallas import tpu as pltpu
from jax.sharding import PartitionSpec as P

LAG = 64

contact_radius = 1.2
contact_width = 0.25
LANES = 128
SUB = 8
MESH = pl.DeviceIdType.MESH


def features_kernel(atoms, coords_ref, ia_ref, ib_ref, out_ref, a_pos, b_pos):
    per_frame = 3 * atoms
    res = coords_ref.shape[1]
    frames = coords_ref.shape[0] // per_frame
    nb = ib_ref.shape[1]
    na = out_ref.shape[1] // nb
    scale = 0.5 / contact_width

    def pick(ids):
        hot = lax.broadcasted_iota(jnp.int32, (res, ids.shape[1]), 0) == ids
        return jnp.dot(
            coords_ref[...], hot.astype(jnp.float32),
            precision=lax.Precision.HIGHEST, preferred_element_type=jnp.float32,
        ) * scale

    a_pos[...] = pick(ia_ref[...])
    b_pos[...] = pick(ib_ref[...])

    def frame_tile(tile, _):
        base = tile * (SUB * per_frame)

        def spread(a, _):
            where = jnp.full((SUB, LANES), a, jnp.int32)
            total = jnp.zeros((SUB, nb), jnp.float32)
            for p in range(atoms):
                left = [
                    jnp.take_along_axis(
                        a_pos[pl.ds(base + c * atoms + p, SUB, stride=per_frame), :], where, axis=1
                    )
                    for c in range(3)
                ]
                part = None
                for q in range(atoms):
                    square = None
                    for c in range(3):
                        d = left[c] - b_pos[pl.ds(base + c * atoms + q, SUB, stride=per_frame), :]
                        square = d * d if square is None else square + d * d
                    square = jnp.maximum(square, 1e-30)
                    half = jnp.tanh(scale * contact_radius - square * lax.rsqrt(square))
                    part = half if part is None else part + half
                total = total + (part + float(atoms))
            out_ref[pl.ds(pl.multiple_of(tile * SUB, SUB), SUB), pl.ds(pl.multiple_of(a * nb, LANES), nb)] = (
                total * (0.5 / atoms)
            )
            return 0

        lax.fori_loop(0, na, spread, 0)
        return 0

    lax.fori_loop(0, frames // SUB, frame_tile, 0)


def features(coords, index_a, set_b):
    frames, comps, atoms, res = coords.shape
    na, nb = index_a.shape[0], set_b.shape[0]
    ia = jnp.pad(index_a, (0, LANES - na)).reshape(1, LANES)
    vm = pl.BlockSpec(memory_space=pltpu.VMEM)
    return pl.pallas_call(
        functools.partial(features_kernel, atoms),
        out_shape=jax.ShapeDtypeStruct((frames, na * nb), jnp.float32),
        in_specs=[vm, vm, vm],
        out_specs=vm,
        scratch_shapes=[
            pltpu.VMEM((frames * comps * atoms, LANES), jnp.float32),
            pltpu.VMEM((frames * comps * atoms, nb), jnp.float32),
        ],
        compiler_params=pltpu.CompilerParams(vmem_limit_bytes=32 * 2**20),
    )(coords.reshape(frames * comps * atoms, res), ia, set_b.reshape(1, nb))


def gather_kernel(T, F, lifted_ref, rows_ref, cols_ref, sums, recv_rows, recv_cols, send_up, send_down,
                  send_x, send_cols, local_sem, sum_send, sum_recv):
    t = lax.axis_index("tm")
    f = lax.axis_index("feat")
    fr = lifted_ref.shape[0]
    width = cols_ref.shape[1]
    pairs = fr * T - LAG

    barrier = pltpu.get_barrier_semaphore()
    for k in range(1, T):
        pl.semaphore_signal(barrier, inc=1, device_id=(lax.rem(t + k, T), f), device_id_type=MESH)
    for k in range(1, F):
        pl.semaphore_signal(barrier, inc=1, device_id=(t, lax.rem(f + k, F)), device_id_type=MESH)

    ids = t * fr + lax.broadcasted_iota(jnp.int32, (fr, 1), 0)
    weight = (ids < pairs).astype(jnp.float32) + (ids >= LAG).astype(jnp.float32)
    sums[t] = jnp.sum(lifted_ref[...] * weight, axis=0, keepdims=True)
    pl.semaphore_wait(barrier, T - 1 + F - 1)

    def sum_copy(k):
        return pltpu.make_async_remote_copy(
            src_ref=sums.at[t], dst_ref=sums.at[t], send_sem=sum_send.at[k], recv_sem=sum_recv.at[t],
            device_id=(lax.rem(t + k, T), f), device_id_type=MESH,
        )

    for k in range(1, T):
        sum_copy(k).start()
    for k in range(1, T):
        other = lax.rem(t + k, T)
        pltpu.make_async_remote_copy(
            src_ref=sums.at[other], dst_ref=sums.at[other], send_sem=sum_send.at[k], recv_sem=sum_recv.at[other],
            device_id=(other, f), device_id_type=MESH,
        ).wait_recv()
    total = sums[0]
    for k in range(1, T):
        total = total + sums[k]
    means = total / (2.0 * pairs)
    rows_ref[pl.ds(pl.multiple_of(t * fr, fr), fr), :] = (lifted_ref[...] - means).astype(jnp.bfloat16)

    m = T // 2
    o = t // 2
    i = t % 2
    owner = t * F // T
    off = pl.multiple_of((t % (T // F)) * width, LANES)
    bits = [1 << b for b in range(F.bit_length() - 1)][::-1]
    r = 0
    for b in bits:
        r = r + b * ((f // b + owner // b) % 2)
    done = []

    def span(block):
        return pl.ds(pl.multiple_of(block * fr, fr), fr)

    def row_copy(block, target, sem):
        return pltpu.make_async_remote_copy(
            src_ref=rows_ref.at[span(block), :], dst_ref=rows_ref.at[span(block), :],
            send_sem=sem.at[block], recv_sem=recv_rows.at[block],
            device_id=(target, f), device_id_type=MESH,
        )

    def col_copy(block, bit, n, from_rows):
        src = rows_ref.at[span(block), pl.ds(off, width)] if from_rows else cols_ref.at[span(block), :]
        peer = f + bit - 2 * bit * ((f // bit) % 2)
        return pltpu.make_async_remote_copy(
            src_ref=src, dst_ref=cols_ref.at[span(block), :],
            send_sem=send_cols.at[n, block], recv_sem=recv_cols.at[block],
            device_id=(t, peer), device_id_type=MESH,
        )

    def local_copy(block):
        return pltpu.make_async_copy(
            rows_ref.at[span(block), pl.ds(off, width)], cols_ref.at[span(block), :], local_sem.at[block]
        )

    def fire(cond, make, wait="send"):
        @pl.when(cond)
        def _():
            make().start()

        done.append((cond, make, wait))

    def cols_from_rows(valid, block):
        for n, bit in enumerate(bits):
            fire(valid & (r == 0), functools.partial(col_copy, block, bit, n, True))
        fire(valid & (r == 0), functools.partial(local_copy, block), "all")

    def cols_onward(valid, block):
        @pl.when(valid & (r != 0))
        def _():
            col_copy(block, bits[0], 0, False).wait_recv()

        for n, bit in enumerate(bits[1:], 1):
            fire(valid & (r != 0) & (r % (2 * bit) == 0), functools.partial(col_copy, block, bit, n, False))

    def at_step(s, lane):
        if s < 0 or s >= m:
            return []
        found = [(o - s >= 0, (o - s) * 2 + lane, True)]
        if s > 0:
            found.append((o + s < m, (o + s) * 2 + lane, False))
        return found

    yes = t >= 0
    for s in range(m + 3):
        for valid, block, below in at_step(s, i):
            if s > 0:
                @pl.when(valid)
                def _():
                    row_copy(block, t, send_x).wait_recv()
            if below or s == 0:
                fire(valid & (o + 1 < m), functools.partial(row_copy, block, t + 2, send_up))
            if not below or s == 0:
                fire(valid & (o >= 1), functools.partial(row_copy, block, t - 2, send_down))
            fire(valid, functools.partial(row_copy, block, o * 2 + 1 - i, send_x))
            cols_from_rows(valid, block)
        for valid, block, below in at_step(s - 1, 1 - i):
            @pl.when(valid)
            def _():
                row_copy(block, t, send_x).wait_recv()

            cols_from_rows(valid, block)
        for valid, block, below in at_step(s - 2, i) + at_step(s - 3, 1 - i):
            cols_onward(valid, block)
    for k in range(1, T):
        sum_copy(k).wait_send()
    for cond, make, wait in done:
        @pl.when(cond)
        def _():
            if wait == "send":
                make().wait_send()
            else:
                make().wait()


def gather(lifted, T, F):
    fr, feats = lifted.shape
    width = feats * F // T
    vm = pl.BlockSpec(memory_space=pltpu.VMEM)
    dma = pltpu.SemaphoreType.DMA
    return pl.pallas_call(
        functools.partial(gather_kernel, T, F),
        out_shape=(
            jax.ShapeDtypeStruct((fr * T, feats), jnp.bfloat16),
            jax.ShapeDtypeStruct((fr * T, width), jnp.bfloat16),
        ),
        in_specs=[vm],
        out_specs=(vm, vm),
        scratch_shapes=[
            pltpu.VMEM((T, 1, feats), jnp.float32),
            dma((T,)), dma((T,)), dma((T,)), dma((T,)), dma((T,)), dma((F, T)), dma((T,)), dma((T,)), dma((T,)),
        ],
        compiler_params=pltpu.CompilerParams(
            collective_id=0, has_side_effects=True, vmem_limit_bytes=48 * 2**20
        ),
    )(lifted)


def product_kernel(pairs, rows_ref, cols_ref, c00_ref, c0t_ref, plus_cols, minus_cols, plus_t, minus_t):
    def halves(ref, at):
        early = ref[:pairs, at].astype(jnp.float32)
        later = ref[LAG:, at].astype(jnp.float32)
        return (early + later).astype(jnp.bfloat16), (early - later).astype(jnp.bfloat16)

    width = cols_ref.shape[1]
    step = min(width, 512)

    @pl.when(pl.program_id(0) == 0)
    def _():
        for at in range(0, width, step):
            plus_cols[:, at:at + step], minus_cols[:, at:at + step] = halves(cols_ref, slice(at, at + step))

    plus_rows, minus_rows = halves(rows_ref, slice(None))
    plus_t[...] = plus_rows.T
    minus_t[...] = minus_rows.T
    share = 1.0 / (4.0 * pairs)

    def columns(n, _):
        at = pl.ds(pl.multiple_of(n * step, step), step)
        sum_plus = jnp.dot(plus_t[...], plus_cols[:, at], preferred_element_type=jnp.float32)
        sum_minus = jnp.dot(minus_t[...], minus_cols[:, at], preferred_element_type=jnp.float32)
        c00_ref[:, at] = (sum_plus + sum_minus) * share
        c0t_ref[:, at] = (sum_plus - sum_minus) * share
        return 0

    lax.fori_loop(0, width // step, columns, 0)


def products(rows, cols):
    frames, height = rows.shape
    width = cols.shape[1]
    pairs = frames - LAG
    tile = 512 if frames <= 1024 else 256
    out = jax.ShapeDtypeStruct((height, width), jnp.float32)
    spec = pl.BlockSpec((tile, width), lambda n: (n, 0))
    return pl.pallas_call(
        functools.partial(product_kernel, pairs),
        out_shape=(out, out),
        grid=(height // tile,),
        in_specs=[pl.BlockSpec((frames, tile), lambda n: (0, n)), pl.BlockSpec((frames, width), lambda n: (0, 0))],
        out_specs=(spec, spec),
        scratch_shapes=[pltpu.VMEM((pairs, width), jnp.bfloat16)] * 2 + [pltpu.VMEM((tile, pairs), jnp.bfloat16)] * 2,
        compiler_params=pltpu.CompilerParams(vmem_limit_bytes=56 * 2**20),
    )(rows, cols)


def solution(mesh):
    T, F = mesh.shape["tm"], mesh.shape["feat"]

    def per_device(coords, set_a, set_b):
        rows_a = set_a.shape[0] // F
        index_a = lax.dynamic_slice_in_dim(set_a, lax.axis_index("feat") * rows_a, rows_a)
        lifted = features(coords, index_a, set_b)
        rows, cols = gather(lifted, T, F)
        return products(rows, cols)

    return jax.shard_map(
        per_device,
        mesh=mesh,
        in_specs=(P("tm", None, None, None), P(), P()),
        out_specs=(P("feat", "tm"), P("feat", "tm")),
        check_vma=False,
    )
```

```python
import functools

import jax
import jax.numpy as jnp
from jax import lax
from jax.experimental import pallas as pl
from jax.experimental.pallas import tpu as pltpu
from jax.sharding import PartitionSpec as P

LAG = 64

contact_radius = 1.2
contact_width = 0.25
LANES = 128
SUB = 8
CHUNKS = 4
MESH = pl.DeviceIdType.MESH


def pick_kernel(coords_ref, ia_ref, ib_ref, a_ref, b_ref, a_all, b_all):
    tiles, per_frame = a_ref.shape[:2]
    res = coords_ref.shape[1]
    scale = 0.5 / contact_width
    hot = jnp.concatenate(
        [
            (lax.broadcasted_iota(jnp.int32, (res, LANES), 0) == ref[...]).astype(jnp.bfloat16)
            for ref in (ia_ref, ib_ref)
        ],
        axis=1,
    )

    def one(tile, _):
        count = SUB * per_frame
        x = coords_ref[pl.ds(pl.multiple_of(tile * count, SUB), count), :]
        high = x.astype(jnp.bfloat16)
        rest = x - high.astype(jnp.float32)
        middle = rest.astype(jnp.bfloat16)
        low = (rest - middle.astype(jnp.float32)).astype(jnp.bfloat16)
        got = jnp.dot(low, hot, preferred_element_type=jnp.float32)
        got = got + jnp.dot(middle, hot, preferred_element_type=jnp.float32)
        got = (got + jnp.dot(high, hot, preferred_element_type=jnp.float32)) * scale
        a_all[...] = got[:, :LANES]
        b_all[...] = got[:, LANES:]
        for k in range(per_frame):
            a_ref[tile, k] = a_all[pl.ds(k, SUB, stride=per_frame), :]
            b_ref[tile, k] = b_all[pl.ds(k, SUB, stride=per_frame), :]
        return 0

    lax.fori_loop(0, tiles, one, 0)


def pick(coords, index_a, set_b):
    frames, comps, atoms, res = coords.shape
    na, nb = index_a.shape[0], set_b.shape[0]
    ia = jnp.pad(index_a, (0, LANES - na)).reshape(1, LANES)
    vm = pl.BlockSpec(memory_space=pltpu.VMEM)
    out = jax.ShapeDtypeStruct((frames // SUB, comps * atoms, SUB, LANES), jnp.float32)
    return pl.pallas_call(
        pick_kernel,
        out_shape=(out, out),
        in_specs=[vm, vm, vm],
        out_specs=(vm, vm),
        scratch_shapes=[pltpu.VMEM((SUB * comps * atoms, LANES), jnp.float32)] * 2,
        compiler_params=pltpu.CompilerParams(vmem_limit_bytes=16 * 2**20),
    )(coords.reshape(frames * comps * atoms, res), ia, set_b.reshape(1, nb))


def gather_kernel(T, F, chunks, a_ref, b_ref, rows_ref, cols_ref, lifted_ref, spread, sums, recv_rows,
                  recv_cols, send_up, send_down, send_x, send_cols, local_sem, sum_send, sum_recv):
    t = lax.axis_index("tm")
    f = lax.axis_index("feat")
    tiles, per_frame = a_ref.shape[:2]
    atoms = per_frame // 3
    fr, feats = lifted_ref.shape
    wide = feats // chunks
    each = wide // LANES
    width = cols_ref.shape[1]
    pairs = fr * T - LAG
    top = contact_radius * 0.5 / contact_width

    barrier = pltpu.get_barrier_semaphore()
    for k in range(1, T):
        pl.semaphore_signal(barrier, inc=1, device_id=(lax.rem(t + k, T), f), device_id_type=MESH)
    for k in range(1, F):
        pl.semaphore_signal(barrier, inc=1, device_id=(t, lax.rem(f + k, F)), device_id_type=MESH)

    def compute(c, first, count):
        def prepare(n, side):
            tile = first + n // each
            where = jnp.full((per_frame * SUB, LANES), c * each + n % each, jnp.int32)
            got = jnp.take_along_axis(a_ref[tile].reshape(per_frame * SUB, LANES), where, axis=1)
            spread[side] = got.reshape(per_frame, SUB, LANES)

        prepare(0, 0)
        last = count * each - 1

        def one(n, _):
            tile = first + n // each
            prepare(jnp.minimum(n + 1, last), (n + 1) % 2)
            total = None
            for p in range(atoms):
                square = None
                for k in range(3):
                    d = spread[n % 2, k * atoms + p][None] - b_ref[tile, k * atoms:(k + 1) * atoms]
                    square = d * d if square is None else square + d * d
                square = jnp.maximum(square, 1e-30)
                half = jnp.sum(jnp.tanh(top - square * lax.rsqrt(square)), axis=0) + float(atoms)
                total = half if total is None else total + half
            lifted_ref[
                pl.ds(pl.multiple_of(tile * SUB, SUB), SUB),
                pl.ds(pl.multiple_of(c * wide + (n % each) * LANES, LANES), LANES),
            ] = total * (0.5 / atoms)
            return 0

        lax.fori_loop(0, last + 1, one, 0)

    def sum_copy(c, source, k):
        return pltpu.make_async_remote_copy(
            src_ref=sums.at[c, source], dst_ref=sums.at[c, source],
            send_sem=sum_send.at[c, k], recv_sem=sum_recv.at[c, source],
            device_id=(lax.rem(t + k, T), f), device_id_type=MESH,
        )

    def send_sums(c):
        ids = t * fr + lax.broadcasted_iota(jnp.int32, (fr, 1), 0)
        weight = (ids < pairs).astype(jnp.float32) + (ids >= LAG).astype(jnp.float32)
        sums[c, t] = jnp.sum(lifted_ref[:, c * wide:(c + 1) * wide] * weight, axis=0, keepdims=True)
        if c == 0:
            pl.semaphore_wait(barrier, T - 1 + F - 1)
        for k in range(1, T):
            sum_copy(c, t, k).start()

    def center(c):
        for k in range(1, T):
            sum_copy(c, lax.rem(t + k, T), k).wait_recv()
        total = sums[c, 0]
        for k in range(1, T):
            total = total + sums[c, k]
        means = total / (2.0 * pairs)
        at = slice(c * wide, (c + 1) * wide)
        rows_ref[pl.ds(pl.multiple_of(t * fr, fr), fr), at] = (lifted_ref[:, at] - means).astype(jnp.bfloat16)

    m = T // 2
    o = t // 2
    i = t % 2
    owner = t * F // T
    part = t % (T // F)
    bits = [1 << b for b in range(F.bit_length() - 1)][::-1]
    r = 0
    for b in bits:
        r = r + b * ((f // b + owner // b) % 2)
    done = []

    def span(block):
        return pl.ds(pl.multiple_of(block * fr, fr), fr)

    piece = min(wide, width)
    per_chunk = wide // piece

    def row_copy(c, block, target, sem):
        at = rows_ref.at[span(block), pl.ds(c * wide, wide)]
        return pltpu.make_async_remote_copy(
            src_ref=at, dst_ref=at, send_sem=sem.at[c, block], recv_sem=recv_rows.at[c, block],
            device_id=(target, f), device_id_type=MESH,
        )

    def in_rows(g, block):
        return rows_ref.at[span(block), pl.ds(g * piece, piece)]

    def in_cols(g, block):
        return cols_ref.at[span(block), pl.ds(g * piece % width, piece)]

    def col_copy(g, block, bit, n, from_rows):
        peer = f + bit - 2 * bit * ((f // bit) % 2)
        return pltpu.make_async_remote_copy(
            src_ref=in_rows(g, block) if from_rows else in_cols(g, block), dst_ref=in_cols(g, block),
            send_sem=send_cols.at[n, g, block], recv_sem=recv_cols.at[g, block],
            device_id=(t, peer), device_id_type=MESH,
        )

    def local_copy(g, block):
        return pltpu.make_async_copy(in_rows(g, block), in_cols(g, block), local_sem.at[g, block])

    def fire(cond, make, wait="send"):
        @pl.when(cond)
        def _():
            make().start()

        done.append((cond, make, wait))

    def blocks_of(c):
        for g in range(c * per_chunk, (c + 1) * per_chunk):
            yield g, part == g * piece // width

    def cols_from_rows(c, valid, block):
        for g, mine in blocks_of(c):
            for n, bit in enumerate(bits):
                fire(valid & mine & (r == 0), functools.partial(col_copy, g, block, bit, n, True))
            fire(valid & mine & (r == 0), functools.partial(local_copy, g, block), "all")

    def cols_onward(c, valid, block):
        for g, mine in blocks_of(c):
            here = valid & mine & (r != 0)

            @pl.when(here)
            def _():
                col_copy(g, block, bits[0], 0, False).wait_recv()

            for n, bit in enumerate(bits[1:], 1):
                fire(here & (r % (2 * bit) == 0), functools.partial(col_copy, g, block, bit, n, False))

    def at_step(s, lane):
        if s < 0 or s >= m:
            return []
        found = [(o - s >= 0, (o - s) * 2 + lane, True)]
        if s > 0:
            found.append((o + s < m, (o + s) * 2 + lane, False))
        return found

    def step(c, s):
        if s == 0:
            center(c)
        for valid, block, below in at_step(s, i):
            if s > 0:
                @pl.when(valid)
                def _():
                    row_copy(c, block, t, send_x).wait_recv()
            if below or s == 0:
                fire(valid & (o + 1 < m), functools.partial(row_copy, c, block, t + 2, send_up))
            if not below or s == 0:
                fire(valid & (o >= 1), functools.partial(row_copy, c, block, t - 2, send_down))
            fire(valid, functools.partial(row_copy, c, block, o * 2 + 1 - i, send_x))
            cols_from_rows(c, valid, block)
        for valid, block, below in at_step(s - 1, 1 - i):
            @pl.when(valid)
            def _():
                row_copy(c, block, t, send_x).wait_recv()

            cols_from_rows(c, valid, block)
        for valid, block, below in at_step(s - 2, i) + at_step(s - 3, 1 - i):
            cols_onward(c, valid, block)

    for slot in range(2 * chunks + m + 3):
        c, h = slot // 2, slot % 2
        if c < chunks:
            compute(c, h * (tiles // 2), tiles // 2)
            if h == 1:
                send_sums(c)
        for c in range(chunks):
            s = slot - 2 * c - 2
            if 0 <= s < m + 3:
                step(c, s)
    for c in range(chunks):
        for k in range(1, T):
            sum_copy(c, t, k).wait_send()
    for cond, make, wait in done:
        @pl.when(cond)
        def _():
            if wait == "send":
                make().wait_send()
            else:
                make().wait()


def gather(a_pos, b_pos, na, T, F):
    tiles, per_frame = a_pos.shape[:2]
    fr, feats = tiles * SUB, na * b_pos.shape[3]
    width = feats * F // T
    chunks = CHUNKS if T <= 8 else 4
    pieces = max(chunks, feats // width)
    vm = pl.BlockSpec(memory_space=pltpu.VMEM)
    dma = pltpu.SemaphoreType.DMA
    return pl.pallas_call(
        functools.partial(gather_kernel, T, F, chunks),
        out_shape=(
            jax.ShapeDtypeStruct((fr * T, feats), jnp.bfloat16),
            jax.ShapeDtypeStruct((fr * T, width), jnp.bfloat16),
        ),
        in_specs=[vm, vm],
        out_specs=(vm, vm),
        scratch_shapes=[
            pltpu.VMEM((fr, feats), jnp.float32),
            pltpu.VMEM((2, per_frame, SUB, LANES), jnp.float32),
            pltpu.VMEM((chunks, T, 1, feats // chunks), jnp.float32),
            dma((chunks, T)), dma((pieces, T)), dma((chunks, T)), dma((chunks, T)), dma((chunks, T)),
            dma((F.bit_length(), pieces, T)), dma((pieces, T)), dma((chunks, T)), dma((chunks, T)),
        ],
        compiler_params=pltpu.CompilerParams(
            collective_id=0, has_side_effects=True, vmem_limit_bytes=48 * 2**20
        ),
    )(a_pos, b_pos)


def product_kernel(pairs, rows_ref, cols_ref, c00_ref, c0t_ref, plus_cols, minus_cols, plus_t, minus_t):
    def halves(ref, at):
        early = ref[:pairs, at].astype(jnp.float32)
        later = ref[LAG:, at].astype(jnp.float32)
        return (early + later).astype(jnp.bfloat16), (early - later).astype(jnp.bfloat16)

    width = cols_ref.shape[1]
    step = min(width, 512)

    @pl.when(pl.program_id(0) == 0)
    def _():
        for at in range(0, width, step):
            plus_cols[:, at:at + step], minus_cols[:, at:at + step] = halves(cols_ref, slice(at, at + step))

    plus_rows, minus_rows = halves(rows_ref, slice(None))
    plus_t[...] = plus_rows.T
    minus_t[...] = minus_rows.T
    share = 1.0 / (4.0 * pairs)

    def columns(n, _):
        at = pl.ds(pl.multiple_of(n * step, step), step)
        sum_plus = jnp.dot(plus_t[...], plus_cols[:, at], preferred_element_type=jnp.float32)
        sum_minus = jnp.dot(minus_t[...], minus_cols[:, at], preferred_element_type=jnp.float32)
        c00_ref[:, at] = (sum_plus + sum_minus) * share
        c0t_ref[:, at] = (sum_plus - sum_minus) * share
        return 0

    lax.fori_loop(0, width // step, columns, 0)


def products(rows, cols):
    frames, height = rows.shape
    width = cols.shape[1]
    pairs = frames - LAG
    tile = 512 if frames <= 1024 else 256
    out = jax.ShapeDtypeStruct((height, width), jnp.float32)
    spec = pl.BlockSpec((tile, width), lambda n: (n, 0))
    return pl.pallas_call(
        functools.partial(product_kernel, pairs),
        out_shape=(out, out),
        grid=(height // tile,),
        in_specs=[pl.BlockSpec((frames, tile), lambda n: (0, n)), pl.BlockSpec((frames, width), lambda n: (0, 0))],
        out_specs=(spec, spec),
        scratch_shapes=[pltpu.VMEM((pairs, width), jnp.bfloat16)] * 2 + [pltpu.VMEM((tile, pairs), jnp.bfloat16)] * 2,
        compiler_params=pltpu.CompilerParams(vmem_limit_bytes=56 * 2**20),
    )(rows, cols)


def solution(mesh):
    T, F = mesh.shape["tm"], mesh.shape["feat"]

    def per_device(coords, set_a, set_b):
        rows_a = set_a.shape[0] // F
        index_a = lax.dynamic_slice_in_dim(set_a, lax.axis_index("feat") * rows_a, rows_a)
        a_pos, b_pos = pick(coords, index_a, set_b)
        rows, cols = gather(a_pos, b_pos, rows_a, T, F)
        return products(rows, cols)

    return jax.shard_map(
        per_device,
        mesh=mesh,
        in_specs=(P("tm", None, None, None), P(), P()),
        out_specs=(P("feat", "tm"), P("feat", "tm")),
        check_vma=False,
    )
```
